256 devices in a mesh: view: 4 (over y_lo, core), ctx: 64 (over x, y_hi, z).
Axes of the slice: x: 4, y: 4 (y_hi: 2, y_lo: 2; y = y_hi * 2 + y_lo), z: 8, core: 2. Of those that a mesh axis runs over, the one named last changes fastest.
Arguments:
- q_self: bfloat16 [4, 7168, 1024], P('view', 'ctx'), may hold values from -16 to 16
- k_self: bfloat16 [4, 7168, 1024], P('view', 'ctx'), may hold values from -16 to 16
- v_self: bfloat16 [4, 7168, 1024], P('view', 'ctx'), may hold values from -6 to 6
- q_cross: bfloat16 [4, 7168, 1024], P('view', 'ctx'), may hold values from -16 to 16
- k_cross: bfloat16 [4, 7168, 1024], P('view', 'ctx'), may hold values from -16 to 16
- v_cross: bfloat16 [4, 7168, 1024], P('view', 'ctx'), may hold values from -6 to 6
Outputs:
- block_out: bfloat16 [4, 7168, 1024], P('view', 'ctx')
The draws below stay inside these ranges and needn't reach their ends.
All inputs are finite; a program needn't handle non-finite values.
Results may differ from the reference program's by a relative error of at most 0.01.
Values may be sent and summed in bfloat16 or wider, within the bound.
A program may use at most 128 MiB of HBM per device.

```python
import jax
import jax.numpy as jnp
from jax import lax

H = 8
HEAD = 128
VIEWS = 4
SEQ = 7168
HD = 1024


def background(key, salt, factor):
    values = jnp.clip(jax.random.normal(jax.random.fold_in(key, salt), (VIEWS, SEQ, HD), jnp.float32), -6.0, 6.0)
    return factor * values


def draw_q_self(key, part):
    values = background(key, 11, 2.5)
    return values.astype(jnp.bfloat16)


def draw_k_self(key, part):
    values = background(key, 12, 1.0)
    return values.astype(jnp.bfloat16)


def draw_q_cross(key, part):
    values = background(key, 13, 1.5)
    return values.astype(jnp.bfloat16)


def draw_k_cross(key, part):
    values = background(key, 14, 1.0)
    return values.astype(jnp.bfloat16)


def block_levels(own_key, dims, pieces, low, largest):
    factor_of, own = 1.0, jax.random.fold_in(own_key, 6)
    for axis_at, blocks in pieces:
        steps = jnp.exp(jax.random.uniform(jax.random.fold_in(own, axis_at), (blocks,), jnp.float32, low / len(pieces), largest / len(pieces)))
        factor_of = factor_of * jnp.repeat(steps, dims[axis_at] // blocks).reshape([-1 if axis == axis_at else 1 for axis in range(len(dims))])
    return factor_of


def bell_draw(key, extent, scale, reach, pieces=(), kind=jnp.bfloat16):
    result = scale * jax.random.normal(key, extent, jnp.float32)
    if pieces:
        result = result * block_levels(key, extent, pieces, -0.22, 0.18)
    return jnp.clip(result, -reach, reach).astype(kind)


def setup_inputs(seed: int = 0) -> dict:
    key_of = jax.random.split(jax.random.key(seed), 7)
    return {
        "q_self": draw_q_self(jax.random.fold_in(key_of[6], 71), 0),
        "k_self": draw_k_self(jax.random.fold_in(key_of[6], 71), 0),
        "v_self": bell_draw(key_of[2], (VIEWS, SEQ, HD), 1.0, 6.0, ((0, 4), (1, 64))),
        "q_cross": draw_q_cross(jax.random.fold_in(key_of[6], 71), 0),
        "k_cross": draw_k_cross(jax.random.fold_in(key_of[6], 71), 0),
        "v_cross": bell_draw(key_of[5], (VIEWS, SEQ, HD), 1.0, 6.0, ((0, 4), (1, 64))),
    }


def one_view(arrays):
    queries, key_rows, value_rows = arrays
    score_scale = 1.0 / (HEAD ** 0.5)

    def one_head(head_arrays):
        query_head, key_head, value_head = head_arrays
        scores = jnp.dot(query_head, key_head.T, preferred_element_type=jnp.float32) * score_scale
        row_max = jnp.max(scores, axis=-1, keepdims=True)
        weights_full = jnp.exp(scores - row_max)
        total_weight = jnp.sum(weights_full, axis=-1, keepdims=True)
        weights_raw = weights_full.astype(jnp.bfloat16)
        return jnp.dot(weights_raw, value_head, preferred_element_type=jnp.float32) / total_weight

    split_q = jnp.transpose(queries.reshape(SEQ, H, HEAD), (1, 0, 2))
    split_k = jnp.transpose(key_rows.reshape(SEQ, H, HEAD), (1, 0, 2))
    split_v = jnp.transpose(value_rows.reshape(SEQ, H, HEAD), (1, 0, 2))
    attended = lax.map(one_head, (split_q, split_k, split_v))
    return jnp.transpose(attended, (1, 0, 2)).reshape(SEQ, HD).astype(jnp.bfloat16)


def reference(q_self, k_self, v_self, q_cross, k_cross, v_cross):
    o_self = lax.map(one_view, (q_self, k_self, v_self))
    cross_query = (q_cross.astype(jnp.float32) + o_self.astype(jnp.float32)).astype(jnp.bfloat16)
    score_scale = 1.0 / (HEAD ** 0.5)
    query_four = cross_query.reshape(VIEWS, SEQ, H, HEAD).astype(jnp.float32)
    key_four = k_cross.reshape(VIEWS, SEQ, H, HEAD).astype(jnp.float32)
    value_four = v_cross.reshape(VIEWS, SEQ, H, HEAD).astype(jnp.float32)
    cross_scores = jnp.einsum('atnd,btnd->tnab', query_four, key_four) * score_scale
    cross_scores = cross_scores - jnp.max(cross_scores, axis=-1, keepdims=True)
    weights_full = jnp.exp(cross_scores)
    cross_weights = (weights_full / jnp.sum(weights_full, axis=-1, keepdims=True)).astype(jnp.bfloat16)
    o_cross = jnp.einsum('tnab,btnd->atnd', cross_weights.astype(jnp.float32), value_four).astype(jnp.bfloat16)
    o_cross = o_cross.reshape(VIEWS, SEQ, HD)
    return (o_self.astype(jnp.float32) + o_cross.astype(jnp.float32)).astype(jnp.bfloat16)
```

```python
import functools
import math

import jax
import jax.numpy as jnp
from jax import lax
from jax.experimental import pallas as pl
from jax.experimental.pallas import tpu as pltpu
from jax.sharding import PartitionSpec as P

HEAD = 128
HEADS = 8
ROWS = 112
BLOCK = HEADS * ROWS
TILE = 128
SCALE = 1.0 / math.sqrt(HEAD)
SCALE2 = SCALE * math.log2(math.e)
MESH = pl.DeviceIdType.MESH
NT = (((1,), (1,)), ((), ()))


def kernel(
    q_in, k_in, v_in, qc_in, kc_in, vc_in, out_ref,
    qbuf, kbuf, vbuf, kcb, vcb, qcb, obuf, ohome, acc, mrow, lrow,
    send_a, recv_a, send_x, recv_x, send_p, recv_p, send_c, recv_c, send_o, recv_o, loc,
):
    view = lax.axis_index("view")
    ctx = lax.axis_index("ctx")
    ylo, core = view // 2, view % 2
    x, yhi, z = ctx // 16, (ctx // 8) % 2, ctx % 8
    rest = ctx % 16
    right = ((x + 1) % 4) * 16 + rest
    left = ((x + 3) % 4) * 16 + rest
    partner = ylo * 2 + (1 - core)
    other = (1 - ylo) * 2 + core
    peer_view = ylo * 2 + yhi
    peer_ctx = x * 16 + core * 8
    same = core == yhi

    barrier = pltpu.get_barrier_semaphore()
    for dev in ((view, right), (view, left), (partner, ctx), (other, ctx)):
        pl.semaphore_signal(barrier, inc=1, device_id=dev, device_id_type=MESH)
    for d in range(1, 8):
        pl.semaphore_signal(
            barrier, inc=1, device_id=(peer_view, peer_ctx + (z + d) % 8), device_id_type=MESH
        )

    @pl.when(jnp.logical_not(same))
    def _():
        pl.semaphore_signal(barrier, inc=1, device_id=(peer_view, peer_ctx + z), device_id_type=MESH)

    pl.semaphore_wait(barrier, 11 + (core + yhi) % 2)

    my_rows = pl.ds(pl.multiple_of(z * ROWS, 16), ROWS)

    def spread(n, src, dst):
        for d in range(8):
            h = (z + d) % 8
            piece = src.at[:, pl.ds(pl.multiple_of(h * HEAD, HEAD), HEAD)]

            def remote():
                pltpu.make_async_remote_copy(
                    src_ref=piece, dst_ref=dst, send_sem=send_a.at[n, d], recv_sem=recv_a.at[n],
                    device_id=(peer_view, peer_ctx + h), device_id_type=MESH,
                ).start()

            if d:
                remote()
            else:
                pl.when(jnp.logical_not(same))(remote)

                @pl.when(same)
                def _():
                    pltpu.make_async_copy(piece, dst, recv_a.at[n]).start()

    spread(0, k_in, kbuf.at[0, my_rows, :])
    spread(1, v_in, vbuf.at[0, my_rows, :])
    spread(2, q_in, qbuf.at[my_rows, :])

    def push(src, dst, send, recv, dev):
        copy = pltpu.make_async_remote_copy(
            src_ref=src, dst_ref=dst, send_sem=send, recv_sem=recv, device_id=dev, device_id_type=MESH
        )
        copy.start()
        return copy

    sent = []
    for n, (src, buf) in enumerate(((kc_in, kcb), (vc_in, vcb))):
        sent.append(push(src, buf.at[2], send_c.at[n, 0], recv_c.at[n, 0], (other, ctx)))
        sent.append(push(src, buf.at[1], send_c.at[n, 1], recv_c.at[n, 1], (partner, ctx)))
    own = [
        pltpu.make_async_copy(kc_in, kcb.at[0], loc.at[0]),
        pltpu.make_async_copy(vc_in, vcb.at[0], loc.at[1]),
        pltpu.make_async_copy(qc_in, qcb, loc.at[2]),
    ]
    for copy in own:
        copy.start()

    bufs = (kbuf, vbuf)
    half = BLOCK // 2

    def got(buf, sem):
        pltpu.make_async_copy(buf, buf, sem).wait()

    def share(n, slot):
        sent.append(
            push(bufs[n].at[slot], bufs[n].at[4 + slot], send_p.at[n, slot], recv_p.at[n, slot], (partner, ctx))
        )

    for n in range(2):
        got(bufs[n].at[0], recv_a.at[n])
        sent.append(push(bufs[n].at[0], bufs[n].at[1], send_x.at[n, 0], recv_x.at[n, 0], (view, right)))
        sent.append(push(bufs[n].at[0], bufs[n].at[2], send_x.at[n, 1], recv_x.at[n, 1], (view, left)))
        share(n, 0)

    def relay(n):
        buf = bufs[n]
        got(buf.at[1], recv_x.at[n, 0])
        low = buf.at[1, pl.ds(0, half), :]
        sent.append(push(low, buf.at[3, pl.ds(0, half), :], send_x.at[n, 2], recv_x.at[n, 2], (view, right)))
        share(n, 1)
        got(buf.at[2], recv_x.at[n, 1])
        high = buf.at[2, pl.ds(half, half), :]
        sent.append(push(high, buf.at[3, pl.ds(half, half), :], send_x.at[n, 3], recv_x.at[n, 3], (view, left)))
        share(n, 2)

    def last(n):
        buf = bufs[n]
        got(buf.at[3, pl.ds(0, half), :], recv_x.at[n, 2])
        got(buf.at[3, pl.ds(half, half), :], recv_x.at[n, 3])
        share(n, 3)

    def attend(slot, first=False):
        def step(t, carry):
            rows = pl.ds(pl.multiple_of(t * TILE, TILE), TILE)
            scores = lax.dot_general(
                qbuf[rows, :], kbuf[slot], NT, preferred_element_type=jnp.float32
            )
            top = jnp.max(scores, axis=1, keepdims=True)
            if not first:
                old = mrow[rows, :]
                top = jnp.maximum(old, top)
            weights = jnp.exp2((scores - top) * SCALE2)
            total = jnp.sum(weights, axis=1, keepdims=True)
            update = jnp.dot(
                weights.astype(jnp.bfloat16), vbuf[slot], preferred_element_type=jnp.float32
            )
            if not first:
                fade = jnp.exp2((old - top) * SCALE2)
                total = total + fade * lrow[rows, :]
                update = update + fade * acc[rows, :]
            mrow[rows, :] = top
            lrow[rows, :] = total
            acc[rows, :] = update
            return carry

        lax.fori_loop(0, BLOCK // TILE, step, 0)

    got(qbuf, recv_a.at[2])
    attend(0, first=True)
    relay(0)
    got(kbuf.at[4], recv_p.at[0, 0])
    got(vbuf.at[4], recv_p.at[1, 0])
    attend(4)
    relay(1)
    attend(1)
    last(0)
    attend(2)
    last(1)
    for slot in (5, 6, 3, 7):
        if slot != 3:
            got(kbuf.at[slot], recv_p.at[0, slot - 4])
            got(vbuf.at[slot], recv_p.at[1, slot - 4])
        attend(slot)
    for n, buf in enumerate((kcb, vcb)):
        got(buf.at[2], recv_c.at[n, 0])
        sent.append(push(buf.at[2], buf.at[3], send_c.at[n, 2], recv_c.at[n, 2], (partner, ctx)))

    obuf[...] = (acc[...] / lrow[...]).astype(jnp.bfloat16)

    for d in range(8):
        j = (z + d) % 8
        piece = obuf.at[pl.ds(pl.multiple_of(j * ROWS, 16), ROWS), :]

        def remote():
            pltpu.make_async_remote_copy(
                src_ref=piece, dst_ref=ohome.at[z], send_sem=send_o.at[d], recv_sem=recv_o.at[0],
                device_id=(peer_view, peer_ctx + j), device_id_type=MESH,
            ).start()

        if d:
            remote()
        else:
            pl.when(jnp.logical_not(same))(remote)

            @pl.when(same)
            def _():
                pltpu.make_async_copy(piece, ohome.at[z], recv_o.at[0]).start()

    for copy in own:
        copy.wait()
    for n, buf in enumerate((kcb, vcb)):
        got(buf.at[1], recv_c.at[n, 1])
        got(buf.at[3], recv_c.at[n, 2])
    got(ohome, recv_o.at[0])

    for h in range(HEADS):
        cols = pl.ds(h * HEAD, HEAD)
        o_self = ohome[h].astype(jnp.float32)
        query = (qcb[:, cols].astype(jnp.float32) + o_self).astype(jnp.bfloat16).astype(jnp.float32)
        scores = [
            jnp.sum(query * kcb[b, :, cols].astype(jnp.float32), axis=1, keepdims=True) * SCALE
            for b in range(4)
        ]
        top = jnp.maximum(jnp.maximum(scores[0], scores[1]), jnp.maximum(scores[2], scores[3]))
        parts = [jnp.exp(s - top) for s in scores]
        total = (parts[0] + parts[1]) + (parts[2] + parts[3])
        mixed = 0.0
        for b in range(4):
            weight = (parts[b] / total).astype(jnp.bfloat16).astype(jnp.float32)
            mixed = mixed + weight * vcb[b, :, cols].astype(jnp.float32)
        o_cross = mixed.astype(jnp.bfloat16).astype(jnp.float32)
        out_ref[:, cols] = (o_self + o_cross).astype(jnp.bfloat16)

    for copy in sent:
        copy.wait_send()
    piece = k_in.at[:, pl.ds(0, HEAD)]
    for d in range(8):

        def drain():
            for n in range(3):
                pltpu.make_async_copy(piece, piece, send_a.at[n, d]).wait()
            pltpu.make_async_copy(piece, piece, send_o.at[d]).wait()

        if d:
            drain()
        else:
            pl.when(jnp.logical_not(same))(drain)


def body(*arrays):
    shape = arrays[0].shape
    flat = [a.reshape(ROWS, HEADS * HEAD) for a in arrays]
    b16, f32 = jnp.bfloat16, jnp.float32
    dma = pltpu.SemaphoreType.DMA
    out = pl.pallas_call(
        kernel,
        name="block",
        out_shape=jax.ShapeDtypeStruct((ROWS, HEADS * HEAD), b16),
        in_specs=[pl.BlockSpec(memory_space=pl.ANY)] * 6,
        out_specs=pl.BlockSpec(memory_space=pltpu.VMEM),
        scratch_shapes=[
            pltpu.VMEM((BLOCK, HEAD), b16),
            pltpu.VMEM((8, BLOCK, HEAD), b16),
            pltpu.VMEM((8, BLOCK, HEAD), b16),
            pltpu.VMEM((4, ROWS, HEADS * HEAD), b16),
            pltpu.VMEM((4, ROWS, HEADS * HEAD), b16),
            pltpu.VMEM((ROWS, HEADS * HEAD), b16),
            pltpu.VMEM((BLOCK, HEAD), b16),
            pltpu.VMEM((HEADS, ROWS, HEAD), b16),
            pltpu.VMEM((BLOCK, HEAD), f32),
            pltpu.VMEM((BLOCK, 1), f32),
            pltpu.VMEM((BLOCK, 1), f32),
            dma((3, 8)), dma((3,)),
            dma((2, 4)), dma((2, 4)),
            dma((2, 4)), dma((2, 4)),
            dma((2, 3)), dma((2, 3)),
            dma((8,)), dma((1,)),
            dma((3,)),
        ],
        compiler_params=pltpu.CompilerParams(collective_id=0, has_side_effects=True),
    )(*flat)
    return out.reshape(shape)


def solution(mesh):
    spec = P("view", "ctx", None)
    return jax.shard_map(body, mesh=mesh, in_specs=(spec,) * 6, out_specs=spec, check_vma=False)
```

```python
import math

import jax
import jax.numpy as jnp
from jax import lax
from jax.experimental import pallas as pl
from jax.experimental.pallas import tpu as pltpu
from jax.sharding import PartitionSpec as P

HEAD = 128
HEADS = 8
ROWS = 112
BLOCK = HEADS * ROWS
HALF = BLOCK // 2
SCALE = 1.0 / math.sqrt(HEAD)
SCALE2 = SCALE * math.log2(math.e)
MESH = pl.DeviceIdType.MESH
NT = (((1,), (1,)), ((), ()))

OWN, P_OWN, LEFT, RIGHT, P_LEFT, P_RIGHT, FAR, P_FAR = range(8)
PAIR = {OWN: P_OWN, LEFT: P_LEFT, RIGHT: P_RIGHT, FAR: P_FAR}
ORDER = (1, 7, 2, 6, 3, 5, 4, 0)
PLACE = {0: 0, 1: 1, 7: 2, 2: 3, 6: 4, 3: 5, 5: 6, 4: 7}


def kernel(
    q_in, k_in, v_in, qc_in, kc_in, vc_in, out_ref,
    qbuf, kbuf, vbuf, kcb, vcb, qcb, obuf, ohome, acc, mrow, lrow,
    send_a, recv_a, send_x, recv_x, send_p, recv_p, send_c, recv_c, send_o, recv_o, loc,
):
    view = lax.axis_index("view")
    ctx = lax.axis_index("ctx")
    ylo, core = view // 2, view % 2
    x, yhi, z = ctx // 16, (ctx // 8) % 2, ctx % 8
    rest = ctx % 16
    right = (view, ((x + 1) % 4) * 16 + rest)
    left = (view, ((x + 3) % 4) * 16 + rest)
    partner = (ylo * 2 + (1 - core), ctx)
    other = ((1 - ylo) * 2 + core, ctx)
    peer_view = ylo * 2 + yhi
    peer_ctx = x * 16 + core * 8
    same = core == yhi
    apart = core != yhi
    bufs = (kbuf, vbuf)

    barrier = pltpu.get_barrier_semaphore()
    for d in range(1, 8):
        pl.semaphore_signal(
            barrier, inc=1, device_id=(peer_view, peer_ctx + (z + d) % 8), device_id_type=MESH
        )

    @pl.when(apart)
    def _():
        pl.semaphore_signal(barrier, inc=1, device_id=(peer_view, peer_ctx + z), device_id_type=MESH)

    for dev in (right, left, partner, other):
        pl.semaphore_signal(barrier, inc=1, device_id=dev, device_id_type=MESH)
    pl.semaphore_wait(barrier, 11 + (core + yhi) % 2)

    def push(src, dst, send, recv, dev):
        pltpu.make_async_remote_copy(
            src_ref=src, dst_ref=dst, send_sem=send, recv_sem=recv, device_id=dev, device_id_type=MESH
        ).start()

    def got(buf, sem):
        pltpu.make_async_copy(buf, buf, sem).wait()

    def exchange(d, dev_z, src, dst, send, recv):
        def remote():
            push(src, dst, send, recv, (peer_view, peer_ctx + dev_z))

        if d:
            remote()
        else:
            pl.when(apart)(remote)

            @pl.when(same)
            def _():
                pltpu.make_async_copy(src, dst, recv).start()

    def spread(n, src, dst):
        for d in ORDER:
            h = (z + d) % 8
            exchange(
                d, h,
                src.at[:, pl.ds(pl.multiple_of(h * HEAD, HEAD), HEAD)],
                dst.at[pl.ds(PLACE[d] * ROWS, ROWS), :],
                send_a.at[n, d], recv_a.at[n, PLACE[d] // 4],
            )

    spread(0, k_in, kbuf.at[OWN])
    spread(2, q_in, qbuf)
    spread(1, v_in, vbuf.at[OWN])

    def part(n, slot, side):
        return bufs[n].at[slot, pl.ds(side * HALF, HALF), :]

    def share(n, slot, side):
        push(
            part(n, slot, side), part(n, PAIR[slot], side),
            send_p.at[n, slot, side], recv_p.at[n, slot, side], partner,
        )

    def own_half(n, side):
        got(part(n, OWN, side), recv_a.at[n, side])
        push(part(n, OWN, side), part(n, LEFT, side), send_x.at[n, 0, side], recv_x.at[n, LEFT, side], right)
        push(part(n, OWN, side), part(n, RIGHT, side), send_x.at[n, 1, side], recv_x.at[n, RIGHT, side], left)
        share(n, OWN, side)

    def relay(n, slot, side):
        got(part(n, slot, side), recv_x.at[n, slot, side])
        if (slot, side) == (LEFT, 0):
            push(part(n, LEFT, 0), part(n, FAR, 0), send_x.at[n, 2, 0], recv_x.at[n, FAR, 0], right)
        if (slot, side) == (RIGHT, 1):
            push(part(n, RIGHT, 1), part(n, FAR, 1), send_x.at[n, 2, 1], recv_x.at[n, FAR, 1], left)
        share(n, slot, side)

    def take(n, slot):
        for side in range(2):
            got(part(n, PAIR[slot], side), recv_p.at[n, slot, side])

    own_half(0, 0)
    own_half(0, 1)
    crossed = ((kc_in, kcb), (vc_in, vcb))
    for n, (src, buf) in enumerate(crossed):
        push(src, buf.at[2], send_c.at[n, 0], recv_c.at[n, 0], other)
        push(src, buf.at[1], send_c.at[n, 1], recv_c.at[n, 1], partner)
    own = [
        pltpu.make_async_copy(kc_in, kcb.at[0], loc.at[0]),
        pltpu.make_async_copy(vc_in, vcb.at[0], loc.at[1]),
        pltpu.make_async_copy(qc_in, qcb, loc.at[2]),
    ]
    for copy in own:
        copy.start()
    mrow[...] = jnp.full_like(mrow, -3e38)
    acc[...] = jnp.zeros_like(acc)
    lrow[...] = jnp.zeros_like(lrow)
    relay(0, LEFT, 0)
    relay(0, RIGHT, 0)
    relay(0, LEFT, 1)
    relay(0, RIGHT, 1)
    got(part(0, OWN, 0), recv_a.at[2, 0])
    got(part(0, OWN, 1), recv_a.at[2, 1])

    def top_step(i, carry):
        @pl.when(i == 1)
        def _():
            take(0, OWN)

        @pl.when(i == 3)
        def _():
            relay(0, FAR, 0)
            relay(0, FAR, 1)
            own_half(1, 0)

        @pl.when(i == 4)
        def _():
            take(0, LEFT)
            take(0, RIGHT)

        @pl.when(i == 6)
        def _():
            own_half(1, 1)

        @pl.when(i == 7)
        def _():
            take(0, FAR)

        scores = lax.dot_general(qbuf[...], kbuf[i], NT, preferred_element_type=jnp.float32)
        top = scores[:, :HEAD]
        for j in range(1, BLOCK // HEAD):
            top = jnp.maximum(top, scores[:, j * HEAD : (j + 1) * HEAD])
        mrow[...] = jnp.maximum(mrow[...], top)
        return carry

    lax.fori_loop(0, 8, top_step, 0)
    mrow[...] = jnp.broadcast_to(jnp.max(mrow[...], axis=1, keepdims=True), (BLOCK, HEAD)) * SCALE2

    def sum_step(i, carry):
        @pl.when(i == 1)
        def _():
            take(1, OWN)
            relay(1, LEFT, 0)
            relay(1, RIGHT, 0)

        @pl.when(i == 2)
        def _():
            relay(1, LEFT, 1)
            relay(1, RIGHT, 1)

        @pl.when(i == 4)
        def _():
            take(1, LEFT)
            take(1, RIGHT)
            for n, (_, buf) in enumerate(crossed):
                got(buf.at[2], recv_c.at[n, 0])
                push(buf.at[2], buf.at[3], send_c.at[n, 2], recv_c.at[n, 2], partner)

        @pl.when(i == 5)
        def _():
            relay(1, FAR, 0)
            relay(1, FAR, 1)

        @pl.when(i == 7)
        def _():
            take(1, FAR)

        scores = lax.dot_general(qbuf[...], kbuf[i], NT, preferred_element_type=jnp.float32)
        top = mrow[...]
        weights = [
            jnp.exp2(scores[:, j * HEAD : (j + 1) * HEAD] * SCALE2 - top) for j in range(BLOCK // HEAD)
        ]
        total = weights[0]
        for w in weights[1:]:
            total = total + w
        lrow[...] += total
        weights = jnp.concatenate([w.astype(jnp.bfloat16) for w in weights], axis=1)
        acc[...] += jnp.dot(weights, vbuf[i], preferred_element_type=jnp.float32)
        return carry

    lax.fori_loop(0, 8, sum_step, 0)
    obuf[...] = (acc[...] / jnp.sum(lrow[...], axis=1, keepdims=True)).astype(jnp.bfloat16)

    for d in ORDER:
        exchange(
            d, (z + 8 - d) % 8,
            obuf.at[pl.ds(PLACE[d] * ROWS, ROWS), :], ohome.at[z],
            send_o.at[d], recv_o.at[0],
        )

    for copy in own:
        copy.wait()
    for n, (_, buf) in enumerate(crossed):
        got(buf.at[1], recv_c.at[n, 1])
        got(buf.at[3], recv_c.at[n, 2])
    got(ohome, recv_o.at[0])

    for h in range(HEADS):
        cols = pl.ds(h * HEAD, HEAD)
        o_self = ohome[h].astype(jnp.float32)
        query = (qcb[:, cols].astype(jnp.float32) + o_self).astype(jnp.bfloat16).astype(jnp.float32)
        scores = [
            jnp.sum(query * kcb[b, :, cols].astype(jnp.float32), axis=1, keepdims=True) * SCALE
            for b in range(4)
        ]
        top = jnp.maximum(jnp.maximum(scores[0], scores[1]), jnp.maximum(scores[2], scores[3]))
        parts = [jnp.exp(s - top) for s in scores]
        total = (parts[0] + parts[1]) + (parts[2] + parts[3])
        mixed = 0.0
        for b in range(4):
            weight = (parts[b] / total).astype(jnp.bfloat16).astype(jnp.float32)
            mixed = mixed + weight * vcb[b, :, cols].astype(jnp.float32)
        o_cross = mixed.astype(jnp.bfloat16).astype(jnp.float32)
        out_ref[:, cols] = (o_self + o_cross).astype(jnp.bfloat16)

    for n in range(2):
        for side in range(2):
            piece = part(n, OWN, side)
            for k in range(3):
                got(piece, send_x.at[n, k, side])
            for slot in PAIR:
                got(piece, send_p.at[n, slot, side])
        for k in range(3):
            got(kcb.at[0], send_c.at[n, k])
    piece = qbuf.at[pl.ds(0, ROWS), :]
    for d in range(8):

        def drain():
            for n in range(3):
                got(piece, send_a.at[n, d])
            got(piece, send_o.at[d])

        if d:
            drain()
        else:
            pl.when(apart)(drain)


def body(*arrays):
    shape = arrays[0].shape
    flat = [a.reshape(ROWS, HEADS * HEAD) for a in arrays]
    b16, f32 = jnp.bfloat16, jnp.float32
    dma = pltpu.SemaphoreType.DMA
    out = pl.pallas_call(
        kernel,
        name="block",
        out_shape=jax.ShapeDtypeStruct((ROWS, HEADS * HEAD), b16),
        in_specs=[pl.BlockSpec(memory_space=pl.ANY)] * 6,
        out_specs=pl.BlockSpec(memory_space=pltpu.VMEM),
        scratch_shapes=[
            pltpu.VMEM((BLOCK, HEAD), b16),
            pltpu.VMEM((8, BLOCK, HEAD), b16),
            pltpu.VMEM((8, BLOCK, HEAD), b16),
            pltpu.VMEM((4, ROWS, HEADS * HEAD), b16),
            pltpu.VMEM((4, ROWS, HEADS * HEAD), b16),
            pltpu.VMEM((ROWS, HEADS * HEAD), b16),
            pltpu.VMEM((BLOCK, HEAD), b16),
            pltpu.VMEM((HEADS, ROWS, HEAD), b16),
            pltpu.VMEM((BLOCK, HEAD), f32),
            pltpu.VMEM((BLOCK, HEAD), f32),
            pltpu.VMEM((BLOCK, HEAD), f32),
            dma((3, 8)), dma((3, 2)),
            dma((2, 3, 2)), dma((2, 8, 2)),
            dma((2, 8, 2)), dma((2, 8, 2)),
            dma((2, 3)), dma((2, 3)),
            dma((8,)), dma((1,)),
            dma((3,)),
        ],
        compiler_params=pltpu.CompilerParams(collective_id=0, has_side_effects=True),
    )(*flat)
    return out.reshape(shape)


def solution(mesh):
    spec = P("view", "ctx", None)
    return jax.shard_map(body, mesh=mesh, in_specs=(spec,) * 6, out_specs=spec, check_vma=False)
```
